32 devices in a mesh: grp: 16 (over z, y, x), tp: 2 (over core).
Axes of the slice: x: 2, y: 2, z: 4, core: 2. Of those that a mesh axis runs over, the one named last changes fastest.
Arguments:
- qkv: bfloat16 [3, 16384, 1408], P(None, 'grp', 'tp'), as said below
- segments: int32 [16, 1024], P('grp'), may hold values from 0 to 255, as said below
- links: int32 [16], P('grp'), may hold values 0 or 1
- owners: int32 [16, 16, 1], P('grp'), may hold values from 0 to 15; in each aligned block of 16 rows (0 to 15, 16 to 31, ..., all dimensions but the last counted through in order) at most 2 rows name the same one
- merge_weight: bfloat16 [4, 1408, 1408], P(None, 'tp'), may hold values from -0.078125 to 0.078125
- norm_gain: float32 [1408], replicated, may hold values from 0.1 to 1.9
- norm_bias: float32 [1408], replicated, may hold values from -3 to 3
- next_weight: bfloat16 [1408, 4224], P(None, 'tp'), may hold values from -0.15625 to 0.15625
Outputs:
- next_qkv: bfloat16 [16, 512, 4224], P('grp', None, 'tp')
The draws below stay inside these ranges and needn't reach their ends.
Inputs may be any that keep to these rules, and one draw needn't show every extreme that they name: `qkv`: entries lie within -6 to 6. Within a row ids start at 0 and never fall; the 4 patches of one merged window share an id; a row has three or more segments; its first and its last segment hold at most 256 patches each, and in some row the first, in some row the last, holds exactly 256. `owners`: in each group's 16 blocks no owner appears more than 2 times, and some owner appears exactly 2 times.
All inputs are finite; a program needn't handle non-finite values. No bound on the sum of `links` on one device may be relied on, other than what follows from the above.
Results may differ from the reference program's by a relative error of at most 0.0062.
Values may be sent and summed in bfloat16 or wider, within the bound.
A program may use at most 192 MiB of HBM per device.

```python
import math
import jax
import jax.numpy as jnp
import numpy as np
from jax import lax

H = 16
DH = 88
L = 1024
WIN = 4
CAP = 2
D = 1408
NG = 16
TOKENS = 16384
RIM = 256
NBLK = 16


def draw_qkv(key, part):
    key = jax.random.fold_in(key, 17)
    key_base = jax.random.fold_in(key, 0)
    result = jax.random.truncated_normal(key_base, -4.0, 4.0, (3, TOKENS, D), jnp.float32)
    return result.astype(jnp.bfloat16)


def draw_segments(key, part):
    key = jax.random.fold_in(key, 29)
    key_first = jax.random.fold_in(key, 0)
    key_last = jax.random.fold_in(key, 1)
    key_row_a = jax.random.fold_in(key, 2)
    key_inner = jax.random.fold_in(key, 4)
    unit_count = L // WIN
    rim_units = RIM // WIN
    first_len = jax.random.randint(key_first, (NG,), 1, rim_units + 1)
    last_len = jax.random.randint(key_last, (NG,), 1, rim_units + 1)
    row_index = jnp.arange(NG)
    busy_row = jax.random.randint(key_row_a, (), 0, NG)
    first_row = (busy_row + 1) % NG
    last_row = (busy_row + 2) % NG
    first_len = jnp.where(row_index == first_row, rim_units, first_len)
    last_len = jnp.where(row_index == last_row, rim_units, last_len)
    position = jnp.arange(unit_count)[None, :]
    inner = jax.random.randint(key_inner, (NG, unit_count), 0, 32) == 0
    inner = jnp.logical_and(inner, jnp.logical_and(position > first_len[:, None], position < unit_count - last_len[:, None]))
    starts = jnp.logical_or(inner, jnp.logical_or(position == first_len[:, None], position == unit_count - last_len[:, None]))
    starts = jnp.where(row_index[:, None] == busy_row, position >= 1, starts)
    unit_ids = jnp.cumsum(starts.astype(jnp.int32), axis=1)
    return jnp.repeat(unit_ids, WIN, axis=1).astype(jnp.int32)


def plant(values, key, smallest, largest):
    dims = values.shape
    place = [jax.random.randint(jax.random.fold_in(key, axis), (), 0, dims[axis]) for axis in range(len(dims))]
    values = values.at[tuple(place)].set(smallest)
    longest = dims.index(max(dims))
    place[longest] = (place[longest] + 1) % dims[longest]
    return values.at[tuple(place)].set(largest)


def level_of(rng, extent, cuts, least, largest):
    def one(dim, blocks):
        draws = jax.random.uniform(jax.random.fold_in(jax.random.fold_in(rng, 6), dim), (blocks,), jnp.float32, least / len(cuts), largest / len(cuts))
        return jnp.repeat(jnp.exp(draws), extent[dim] // blocks).reshape((-1,) + (1,) * (len(extent) - dim - 1))

    loudness = one(*cuts[0])
    for cut in cuts[1:]:
        loudness = loudness * one(*cut)
    return loudness


def deal_out(key, own, number, rows, amount, top, limit, lean):
    sequence = jax.random.permutation(key, amount)
    crowded, usual = load_shares(amount, rows * top, limit, lean, True), load_shares(amount, rows * top, limit, lean, False)
    places = jnp.arange(amount)

    def named(tallies, offset_by):
        used = int((tallies > 0).sum())
        fixed = max(1, used // 4)
        shifted = fixed + (places - fixed + offset_by * (used - fixed)) % max(1, amount - fixed)
        return jnp.zeros((amount,), jnp.int32).at[sequence[jnp.where(places < fixed, places, shifted)]].set(jnp.asarray(tallies, jnp.int32))

    tallies = jnp.where(number % 4 == 0, named(crowded, number // 4), named(usual, number - number // 4 - 1))
    mixed = jax.random.permutation(jax.random.fold_in(own, 3), amount)
    source_of, receiver = mixed[0:amount // 2 * 2:2], mixed[1:amount // 2 * 2:2]
    margin = jnp.minimum(tallies[source_of] - 1, limit - tallies[receiver]) // 2
    margin = jnp.where((source_of == sequence[0]) | (receiver == sequence[0]) | (tallies[receiver] == 0), 0, jnp.maximum(margin, 0))
    shifted = jax.random.randint(jax.random.fold_in(own, 4), (amount // 2,), 0, 1 << 20) % (margin + 1)
    tallies = tallies.at[source_of].add(-shifted).at[receiver].add(shifted)
    labels = jnp.searchsorted(jnp.cumsum(tallies), jnp.arange(rows * top), side="right").astype(jnp.int32)
    grid = labels.reshape(top, rows).T
    grid = grid[jax.random.permutation(jax.random.fold_in(own, 1), rows)]
    offset_by = jax.random.randint(jax.random.fold_in(own, 2), (rows, 1), 0, top)
    return jnp.take_along_axis(grid, (jnp.arange(top)[None, :] + offset_by) % top, axis=1)


def load_shares(count, total, limit, lean, full):
    portions = [(1 << 20) // math.isqrt(standing ** lean) + 1 for standing in range(1, count + 1)]
    largest = limit if full else min(limit, max(-(-total // count), total * portions[0] // sum(portions)))
    least = 1 if total - largest >= count - 1 else 0
    given, spare = [largest] + [least] * (count - 1), total - largest - least * (count - 1)
    while spare > 0:
        free = [i for i in range(1, count) if given[i] < largest] or [i for i in range(1, count) if given[i] < limit]
        whole, left = sum([portions[i] for i in free]), spare
        for i in free:
            addition = min(limit - given[i], max(1, left * portions[i] // whole), spare)
            given[i] = given[i] + addition
            spare = spare - addition
    return np.array(given)


def noise(key, extent, width, bound, shards=(), held_as=jnp.bfloat16):
    loudness = level_of(key, extent, shards, -0.22, 0.18) if shards else 1.0
    values = jax.random.normal(key, extent, jnp.float32) * width * loudness
    return jnp.minimum(jnp.maximum(values, -bound), bound).astype(held_as)


def setup_inputs(seed: int = 0) -> dict:
    seeds = jax.random.split(jax.random.key(seed), 9)
    qkv = draw_qkv(jax.random.fold_in(seeds[8], 71), 0)
    segments = draw_segments(jax.random.fold_in(seeds[8], 71), 0)
    links = plant((jax.random.randint(seeds[2], (NG,), 0, 2) < 1).astype(jnp.int32), jax.random.fold_in(seeds[2], 1), 0, 1)
    owners_keys = jax.random.split(jax.random.fold_in(seeds[3], 1), NG * NBLK // NBLK)
    owners_turns = jax.random.permutation(jax.random.fold_in(seeds[3], 3), NG * NBLK // NBLK)
    owners = jax.vmap(lambda own, number: deal_out(jax.random.fold_in(seeds[3], 2), own, number, NBLK, NG, 1, CAP, 1))(owners_keys, owners_turns).reshape((NG, NBLK, 1))
    merge_weight = noise(seeds[4], (WIN, D, D), (WIN * D) ** -0.5, 0.078125, ((1, 2),))
    norm_gain = jnp.clip(1.0 + 0.18 * jax.random.normal(seeds[5], (D,), jnp.float32), 0.1, 1.9)
    norm_bias = noise(seeds[6], (D,), 0.5, 3.0, (), jnp.float32)
    next_weight = noise(seeds[7], (D, 3 * D), D ** -0.5, 0.15625, ((1, 2),))
    return dict(qkv=qkv, segments=segments, links=links, owners=owners, merge_weight=merge_weight, norm_gain=norm_gain, norm_bias=norm_bias, next_weight=next_weight)


def reference(qkv, segments, links, owners, merge_weight, norm_gain, norm_bias, next_weight):
    score_scale = 1.0 / math.sqrt(DH)
    group_total = segments.shape[0]
    row_len = segments.shape[1]
    model_width = H * DH
    first_seg = segments == segments[:, :1]
    last_seg = segments == segments[:, row_len - 1:]
    linked = jnp.logical_and(links > 0, jnp.arange(group_total) < group_total - 1)
    empty_row = jnp.zeros((1, row_len), dtype=bool)
    left_keys = jnp.concatenate([empty_row, jnp.logical_and(last_seg, linked[:, None])[:-1]], axis=0)
    right_keys = jnp.logical_and(jnp.concatenate([first_seg[1:], empty_row], axis=0), linked[:, None])
    padded = jnp.pad(qkv.reshape(3, group_total, row_len, H, DH), ((0, 0), (1, 1), (0, 0), (0, 0), (0, 0)))

    def attend(group):
        group = group.astype(jnp.int32)
        window = lax.dynamic_slice_in_dim(padded, group, 3, axis=1)
        queries = window[0, 1].astype(jnp.float32)
        all_keys = window[1].reshape(3 * row_len, H, DH).astype(jnp.float32)
        all_values = window[2].reshape(3 * row_len, H, DH).astype(jnp.float32)
        seg_ids = segments[group]
        same_seg = seg_ids[:, None] == seg_ids[None, :]
        left_ok = jnp.logical_and(first_seg[group][:, None], left_keys[group][None, :])
        right_ok = jnp.logical_and(last_seg[group][:, None], right_keys[group][None, :])
        allowed = jnp.concatenate([left_ok, same_seg, right_ok], axis=1)
        scores = jnp.einsum('qhd,khd->hqk', queries, all_keys) * score_scale
        scores = jnp.where(allowed[None], scores, -jnp.inf)
        row_max = lax.optimization_barrier(jnp.max(scores, axis=2, keepdims=True))
        exp_scores = jnp.exp(scores - row_max)
        weights = (exp_scores / lax.optimization_barrier(jnp.sum(exp_scores, axis=2, keepdims=True))).astype(jnp.bfloat16)
        attended_row = jnp.einsum('hqk,khd->qhd', weights.astype(jnp.float32), all_values)
        return attended_row.astype(jnp.bfloat16).reshape(row_len, model_width)
    attended = lax.map(attend, jnp.arange(group_total))
    merged = jnp.dot(attended.reshape(-1, WIN * model_width), merge_weight.reshape(WIN * model_width, model_width), preferred_element_type=jnp.float32)
    feature_mean = lax.optimization_barrier(jnp.mean(merged, axis=1, keepdims=True))
    variance = lax.optimization_barrier(jnp.mean(merged * merged, axis=1, keepdims=True)) - feature_mean * feature_mean
    normed = ((merged - feature_mean) * lax.rsqrt(variance + 1e-05) * norm_gain + norm_bias).astype(jnp.bfloat16)
    owner_ids = owners[:, :, 0].astype(jnp.int32)
    block_total = owner_ids.shape[1]
    block_index = jnp.arange(block_total)
    earlier = block_index[:, None] > block_index[None, :]
    slot_rank = lax.optimization_barrier(jnp.sum(jnp.logical_and(owner_ids[:, :, None] == owner_ids[:, None, :], earlier[None]).astype(jnp.int32), axis=2))
    block_rows = row_len // WIN // block_total
    slot_count = group_total * CAP * block_rows
    slot_base = (jnp.arange(group_total, dtype=jnp.int32)[:, None] * CAP + slot_rank) * block_rows
    slot_index = (slot_base[:, :, None] + jnp.arange(block_rows, dtype=jnp.int32)[None, None, :]).astype(jnp.int32)
    routed = jnp.zeros((group_total, slot_count, model_width), jnp.bfloat16)
    routed = routed.at[owner_ids[:, :, None], slot_index].set(normed.reshape(group_total, block_total, block_rows, model_width))
    projected = jnp.dot(routed.reshape(-1, model_width), next_weight, preferred_element_type=jnp.float32).astype(jnp.bfloat16)
    return projected.reshape(group_total, slot_count, 3 * model_width)
```

```python
import functools
import math

import jax
import jax.numpy as jnp
from jax import lax
from jax.experimental import pallas as pl
from jax.experimental.pallas import tpu as pltpu
from jax.sharding import PartitionSpec as P

DH = 88
WIN = 4
CAP = 2
TILE = 128
EPS = 1e-05
NEG = -1e30
SCALE2 = math.log2(math.e) / math.sqrt(DH)


def shifted(block, axis, distance):
    devices = range(lax.axis_size(axis))
    route = [(i - distance, i) for i in devices if i - distance in devices]
    return lax.ppermute(block, axis, route)


def swapped(block, axis):
    return lax.ppermute(block, axis, [(0, 1), (1, 0)])


def windows(width):
    spans = []
    for head in range(width // DH):
        low, high = head * DH, head * DH + DH
        spans.append((low, high, low // TILE * TILE, min(width, -(-high // TILE) * TILE)))
    return spans


def head_mask(low, high, start, stop):
    column = start + lax.broadcasted_iota(jnp.int32, (1, stop - start), 1)
    return jnp.logical_and(column >= low, column < high)


def attend_heads(width, read_query, key_parts, bias_parts, value_parts, write):
    pieces = {}
    for low, high, start, stop in windows(width):
        mask = head_mask(low, high, start, stop)
        query = read_query(start, stop) * mask.astype(jnp.float32).astype(jnp.bfloat16)
        scores = [
            lax.dot_general(
                query, keys(start, stop), (((1,), (1,)), ((), ())), preferred_element_type=jnp.float32
            )
            * SCALE2
            + bias
            for keys, bias in zip(key_parts, bias_parts)
        ]
        top = jnp.max(scores[0], axis=1, keepdims=True)
        for part in scores[1:]:
            top = jnp.maximum(top, jnp.max(part, axis=1, keepdims=True))
        weights = [jnp.exp2(part - top) for part in scores]
        total = jnp.sum(weights[0], axis=1, keepdims=True)
        for part in weights[1:]:
            total = total + jnp.sum(part, axis=1, keepdims=True)
        mixed = None
        for part, values in zip(weights, value_parts):
            term = jnp.dot(
                part.astype(jnp.bfloat16), values(start, stop), preferred_element_type=jnp.float32
            )
            mixed = term if mixed is None else mixed + term
        mixed = mixed * (1.0 / total)
        for at in range(start, stop, TILE):
            end = min(at + TILE, stop)
            piece = mixed[:, at - start : end - start]
            if at in pieces:
                piece = jnp.where(head_mask(low, high, at, end), piece, pieces[at])
            pieces[at] = piece
            if high >= end:
                write(at, end, pieces[at].astype(jnp.bfloat16))


def attention_kernel(edge, row_len, width, sent, *refs):
    if edge:
        seg_smem, counts, qkv, seg_row, seg_col, prev, following, out = refs
    else:
        seg_smem, qkv, seg_row, seg_col, out = refs
    tiles = row_len // TILE
    edge_tiles = sent // TILE

    def one(tile, out_row, neighbour):
        first = seg_smem[0, tile * TILE]
        last = seg_smem[0, tile * TILE + TILE - 1]
        begin, stop = jnp.int32(0), jnp.int32(0)
        for other in range(tiles):
            begin += (seg_smem[0, other * TILE + TILE - 1] < first).astype(jnp.int32)
            stop += (seg_smem[0, other * TILE] <= last).astype(jnp.int32)
        needed = stop - begin
        query_at = pl.multiple_of(tile * TILE, TILE)
        query_ids = seg_col[pl.ds(query_at, TILE), :]

        def run(count):
            key_tile = jnp.minimum(begin, tiles - count)
            key_at = pl.multiple_of(key_tile * TILE, TILE)
            ids = jnp.concatenate([seg_row[pl.ds(key_tile + i, 1), :] for i in range(count)], axis=1)
            bias_parts = [jnp.where(query_ids == ids, 0.0, NEG)]
            key_parts = [lambda a, b: qkv[1, pl.ds(key_at, count * TILE), a:b]]
            value_parts = [lambda a, b: qkv[2, pl.ds(key_at, count * TILE), a:b]]
            if neighbour is not None:
                source, allowed = neighbour
                bias_parts.append(jnp.where(allowed, 0.0, NEG))
                key_parts.append(lambda a, b: source[0, :sent, a:b])
                value_parts.append(lambda a, b: source[1, :sent, a:b])

            def write(a, b, value):
                out[pl.ds(out_row, TILE), a:b] = value

            attend_heads(
                width,
                lambda a, b: qkv[0, pl.ds(query_at, TILE), a:b],
                key_parts,
                bias_parts,
                value_parts,
                write,
            )

        sizes = [size for size in (2, 3, 4) if size < tiles] + [tiles]
        floor = 0
        for size in sizes:
            pl.when(jnp.logical_and(needed > floor, needed <= size))(functools.partial(run, size))
            floor = size

    if not edge:
        @pl.loop(edge_tiles, tiles - edge_tiles)
        def _(tile):
            one(tile, pl.multiple_of((tile - edge_tiles) * TILE, TILE), None)
        return

    slot = lax.broadcasted_iota(jnp.int32, (1, sent), 1)

    @pl.loop(0, edge_tiles)
    def _(tile):
        at = pl.multiple_of(tile * TILE, TILE)
        rows = seg_col[pl.ds(at, TILE), :]
        ok = jnp.logical_and(rows == seg_smem[0, 0], slot >= sent - counts[0])
        one(tile, at, (prev, ok))

    @pl.loop(0, edge_tiles)
    def _(step):
        tile = tiles - edge_tiles + step
        rows = seg_col[pl.ds(pl.multiple_of(tile * TILE, TILE), TILE), :]
        ok = jnp.logical_and(rows == seg_smem[0, row_len - 1], slot < counts[1])
        one(tile, pl.multiple_of((edge_tiles + step) * TILE, TILE), (following, ok))


def run_attention(edge, qkv, segments, sent, extra):
    row_len, width = qkv.shape[1:]
    rows = 2 * sent if edge else row_len - 2 * sent
    smem = pl.BlockSpec(memory_space=pltpu.SMEM)
    vmem = pl.BlockSpec(memory_space=pltpu.VMEM)
    operands = [segments]
    specs = [smem]
    if edge:
        operands.append(extra[0])
        specs.append(smem)
    operands += [qkv, segments.reshape(row_len // TILE, TILE), segments.reshape(row_len, 1)]
    specs += [vmem] * 3
    if edge:
        operands += [extra[1], extra[2]]
        specs += [vmem] * 2
    return pl.pallas_call(
        functools.partial(attention_kernel, edge, row_len, width, sent),
        out_shape=jax.ShapeDtypeStruct((rows, width), jnp.bfloat16),
        in_specs=specs,
        out_specs=vmem,
        compiler_params=pltpu.CompilerParams(vmem_limit_bytes=40 << 20),
        cost_estimate=pl.CostEstimate(
            flops=rows * 512 * width * 6, bytes_accessed=qkv.size * 2, transcendentals=rows * 512 * 8
        ),
        name="edge_attention" if edge else "middle_attention",
    )(*operands)


def norm_pack_kernel(width, mine_ref, other_ref, gain_ref, bias_ref, target_ref, half_ref, out_ref):
    merged = mine_ref[...] + other_ref[...]
    model_width = merged.shape[1]
    mean = jnp.sum(merged, axis=1, keepdims=True) / model_width
    variance = jnp.sum(merged * merged, axis=1, keepdims=True) / model_width - mean * mean
    normed = (merged - mean) * lax.rsqrt(variance + EPS) * gain_ref[...] + bias_ref[...]
    normed = normed.astype(jnp.bfloat16)
    left, right = normed[:, :width], normed[:, width:]
    place = lax.broadcasted_iota(jnp.int32, (out_ref.shape[0], merged.shape[0]), 0)
    place = jnp.where(place == target_ref[...], 1.0, 0.0).astype(jnp.bfloat16)
    half = half_ref[0]

    @pl.when(half == 0)
    def _():
        out_ref[...] = jnp.dot(place, left, preferred_element_type=jnp.float32).astype(jnp.bfloat16)

    @pl.when(half != 0)
    def _():
        out_ref[...] = jnp.dot(place, right, preferred_element_type=jnp.float32).astype(jnp.bfloat16)


def norm_pack(mine, other, gain, bias, target, half, slots):
    width = mine.shape[1] // 2
    vmem = pl.BlockSpec(memory_space=pltpu.VMEM)
    return pl.pallas_call(
        functools.partial(norm_pack_kernel, width),
        out_shape=jax.ShapeDtypeStruct((slots, width), jnp.bfloat16),
        in_specs=[vmem] * 5 + [pl.BlockSpec(memory_space=pltpu.SMEM)],
        out_specs=vmem,
        compiler_params=pltpu.CompilerParams(vmem_limit_bytes=32 << 20),
        name="norm_pack",
    )(mine, other, gain[None], bias[None], target[None], half)


def body(qkv, segments, links, owners, merge_weight, norm_gain, norm_bias, next_weight):
    row_len = qkv.shape[1]
    shard_width = qkv.shape[2]
    model_width = norm_gain.shape[0]
    tp_size = lax.axis_size("tp")
    seg_ids = segments[0]
    linked = links[0] > 0
    sent = row_len // 4
    last_count = jnp.sum((seg_ids == seg_ids[row_len - 1]).astype(jnp.int32))
    first_count = jnp.sum((seg_ids == seg_ids[0]).astype(jnp.int32))
    last_count = jnp.where(linked, last_count, 0)

    def payload(pairs, count):
        mark = jnp.broadcast_to(count.astype(jnp.bfloat16), (2, 16, shard_width))
        return jnp.concatenate([pairs, mark], axis=1)

    prev = shifted(payload(qkv[1:3, row_len - sent :], last_count), "grp", 1)
    following = shifted(payload(qkv[1:3, :sent], first_count), "grp", -1)
    prev_count = prev[0, sent, 0].astype(jnp.int32)
    next_count = jnp.where(linked, following[0, sent, 0].astype(jnp.int32), 0)
    merge_flat = merge_weight.reshape(WIN * shard_width, model_width)

    def merge(attended):
        return jnp.dot(
            attended.reshape(-1, WIN * shard_width), merge_flat, preferred_element_type=jnp.float32
        )

    middle = merge(run_attention(False, qkv, segments, sent, None))
    edges = merge(
        run_attention(True, qkv, segments, sent, (jnp.stack([prev_count, next_count]), prev, following))
    )
    cut = sent // WIN
    partial_sum = jnp.concatenate([edges[:cut], middle, edges[cut:]], axis=0)
    merged_rows = row_len // WIN

    owner_ids = owners[0, :, 0]
    block_count = owner_ids.shape[0]
    group_count = lax.axis_size("grp")
    block_rows = merged_rows // block_count
    block_index = jnp.arange(block_count)
    earlier = block_index[:, None] > block_index[None, :]
    slot_rank = jnp.sum(
        jnp.logical_and(owner_ids[:, None] == owner_ids[None, :], earlier).astype(jnp.int32), axis=1
    )
    target = (owner_ids * CAP + slot_rank)[:, None] * block_rows + jnp.arange(block_rows)[None, :]
    target = target.reshape(merged_rows)
    slots = group_count * CAP * block_rows

    if tp_size == 2:
        half_index = lax.axis_index("tp")
        other = swapped(partial_sum, "tp")
        packed = norm_pack(
            partial_sum, other, norm_gain, norm_bias, target, half_index[None].astype(jnp.int32), slots
        )
        half_width = model_width // 2
        packed = packed.reshape(group_count, CAP * block_rows, half_width)
        arrived = lax.all_to_all(packed, "grp", split_axis=0, concat_axis=0, tiled=True)
        arrived = arrived.reshape(slots, half_width)
        beside = swapped(arrived, "tp")
        left = jnp.where(half_index == 0, arrived, beside)
        right = jnp.where(half_index == 0, beside, arrived)
        routed = jnp.concatenate([left, right], axis=1)
    else:
        merged = lax.psum(partial_sum, "tp")
        mean = jnp.mean(merged, axis=1, keepdims=True)
        variance = jnp.mean(merged * merged, axis=1, keepdims=True) - mean * mean
        normed = (merged - mean) * lax.rsqrt(variance + EPS) * norm_gain + norm_bias
        normed = normed.astype(jnp.bfloat16)
        placing = (jnp.arange(slots)[:, None] == target[None, :]).astype(jnp.bfloat16)
        packed = jnp.dot(placing, normed, preferred_element_type=jnp.float32).astype(jnp.bfloat16)
        packed = packed.reshape(group_count, CAP * block_rows, model_width)
        routed = lax.all_to_all(packed, "grp", split_axis=0, concat_axis=0, tiled=True)
        routed = routed.reshape(slots, model_width)
    projected = jnp.dot(routed, next_weight, preferred_element_type=jnp.float32)
    return projected.astype(jnp.bfloat16)[None]


def solution(mesh):
    placed = (
        P(None, "grp", "tp"),
        P("grp", None),
        P("grp"),
        P("grp", None, None),
        P(None, "tp", None),
        P(),
        P(),
        P(None, "tp"),
    )
    return jax.shard_map(
        body, mesh=mesh, in_specs=placed, out_specs=P("grp", None, "tp"), check_vma=False
    )
```

```python
import functools
import math

import jax
import jax.numpy as jnp
from jax import lax
from jax.experimental import pallas as pl
from jax.experimental.pallas import tpu as pltpu
from jax.sharding import PartitionSpec as P

DH = 88
WIN = 4
CAP = 2
TILE = 128
PACK = 16
EPS = 1e-05
NEG = -1e30
SCALE2 = math.log2(math.e) / math.sqrt(DH)


def shifted(block, axis, distance):
    devices = range(lax.axis_size(axis))
    route = [(i - distance, i) for i in devices if i - distance in devices]
    return lax.ppermute(block, axis, route)


def swapped(block, axis):
    return lax.ppermute(block, axis, [(0, 1), (1, 0)])


def head_scores(query, keys, bias):
    scores = lax.dot_general(keys, query, (((0,), (0,)), ((), ())), preferred_element_type=jnp.float32)
    return scores * SCALE2 + bias


def attend_heads(width, read_query, key_parts, bias_parts, value_parts):
    pieces = []
    for head in range(width // DH):
        low = head * DH
        start = low // PACK * PACK
        stop = -(-(low + DH) // PACK) * PACK
        row = start + lax.broadcasted_iota(jnp.int32, (stop - start, 1), 0)
        inside = jnp.logical_and(row >= low, row < low + DH)
        query = read_query(start, stop)
        query = jnp.where(inside, query.astype(jnp.float32), 0.0).astype(jnp.bfloat16)
        scores = [head_scores(query, keys(start, stop), bias) for keys, bias in zip(key_parts, bias_parts)]
        top = jnp.max(scores[0], axis=0, keepdims=True)
        for part in scores[1:]:
            top = jnp.maximum(top, jnp.max(part, axis=0, keepdims=True))
        weights = [jnp.exp2(part - top) for part in scores]
        total = jnp.sum(weights[0], axis=0, keepdims=True)
        for part in weights[1:]:
            total = total + jnp.sum(part, axis=0, keepdims=True)
        scale = 1.0 / total
        mixed = None
        for part, values in zip(weights, value_parts):
            term = jnp.dot(
                values(start, stop), (part * scale).astype(jnp.bfloat16), preferred_element_type=jnp.float32
            )
            mixed = term if mixed is None else mixed + term
        pieces.append(mixed[low - start : low - start + DH])
    return jnp.concatenate(pieces, axis=0)


def attention_kernel(edge, row_len, width, sent, *refs):
    if edge:
        seg_smem, qkv, seg_row, seg_col, merge_hbm, links, prev, following, middle, out = refs[:10]
    else:
        seg_smem, qkv, seg_row, seg_col, merge_hbm, out = refs[:6]
    attended, merge_vmem, merge_sem = refs[-3:]
    tiles = row_len // TILE
    edge_tiles = sent // TILE
    tokens = TILE // WIN
    fetch = pltpu.make_async_copy(merge_hbm, merge_vmem, merge_sem)
    fetch.start()
    ordered = lax.broadcasted_iota(jnp.int32, (TILE, TILE), 0)
    ordered = (ordered % tokens) * WIN + ordered // tokens
    order = (ordered == lax.broadcasted_iota(jnp.int32, (TILE, TILE), 1)).astype(jnp.float32)
    order = order.astype(jnp.bfloat16)

    def one(tile, out_row, neighbour):
        first = seg_smem[0, tile * TILE]
        last = seg_smem[0, tile * TILE + TILE - 1]
        begin, stop = jnp.int32(0), jnp.int32(0)
        for other in range(tiles):
            begin += (seg_smem[0, other * TILE + TILE - 1] < first).astype(jnp.int32)
            stop += (seg_smem[0, other * TILE] <= last).astype(jnp.int32)
        needed = stop - begin
        query_at = pl.multiple_of(tile * TILE, TILE)
        query_ids = seg_row[pl.ds(tile, 1), :]

        def run(count):
            key_at = pl.multiple_of(jnp.minimum(begin, tiles - count) * TILE, TILE)
            key_ids = seg_col[pl.ds(key_at, count * TILE), :]
            bias_parts = [jnp.where(key_ids == query_ids, 0.0, NEG)]
            key_parts = [lambda a, b: qkv[1, a:b, pl.ds(key_at, count * TILE)]]
            value_parts = [lambda a, b: qkv[2, a:b, pl.ds(key_at, count * TILE)]]
            if neighbour is not None:
                source, segment, open_link = neighbour
                marks = jnp.transpose(source[0, width : width + PACK, :].astype(jnp.float32))[:, :1]
                wanted = jnp.logical_and(query_ids == segment, open_link).astype(jnp.float32)
                bias_parts.append(jnp.where(marks * wanted > 0.5, 0.0, NEG))
                key_parts.append(lambda a, b: source[0, a:b, :])
                value_parts.append(lambda a, b: source[1, a:b, :])
            mixed = attend_heads(
                width,
                lambda a, b: qkv[0, a:b, pl.ds(query_at, TILE)],
                key_parts,
                bias_parts,
                value_parts,
            )
            turned = lax.dot_general(
                order,
                mixed.astype(jnp.bfloat16),
                (((1,), (1,)), ((), ())),
                preferred_element_type=jnp.float32,
            ).astype(jnp.bfloat16)
            for j in range(WIN):
                attended[j, pl.ds(out_row, tokens), :] = turned[j * tokens : (j + 1) * tokens]

        sizes = [size for size in (2, 3, 4) if size < tiles] + [tiles]
        floor = 0
        for size in sizes:
            pl.when(jnp.logical_and(needed > floor, needed <= size))(functools.partial(run, size))
            floor = size

    if edge:
        @pl.loop(0, edge_tiles)
        def _(tile):
            one(tile, pl.multiple_of(tile * tokens, tokens), (prev, seg_smem[0, 0], True))

        @pl.loop(0, edge_tiles)
        def _(step):
            one(
                tiles - edge_tiles + step,
                pl.multiple_of((edge_tiles + step) * tokens, tokens),
                (following, seg_smem[0, row_len - 1], links[0] > 0),
            )
    else:
        @pl.loop(edge_tiles, tiles - edge_tiles)
        def _(tile):
            one(tile, pl.multiple_of((tile - edge_tiles) * tokens, tokens), None)

    fetch.wait()
    merged = jnp.dot(attended[0], merge_vmem[0], preferred_element_type=jnp.float32)
    for j in range(1, WIN):
        merged += jnp.dot(attended[j], merge_vmem[j], preferred_element_type=jnp.float32)
    if edge:
        half = merged.shape[0] // 2
        out[:half, :] = merged[:half]
        out[half : half + middle.shape[0], :] = middle[...]
        out[half + middle.shape[0] :, :] = merged[half:]
    else:
        out[...] = merged


def run_attention(edge, qkv, segments, merge_weight, sent, extra):
    width, row_len = qkv.shape[1:]
    model_width = merge_weight.shape[2]
    rows = 2 * sent if edge else row_len - 2 * sent
    smem = pl.BlockSpec(memory_space=pltpu.SMEM)
    vmem = pl.BlockSpec(memory_space=pltpu.VMEM)
    operands = [
        segments,
        qkv,
        segments.reshape(row_len // TILE, TILE),
        segments.reshape(row_len, 1),
        merge_weight,
    ]
    specs = [smem, vmem, vmem, vmem, pl.BlockSpec(memory_space=pl.ANY)]
    if edge:
        operands += list(extra)
        specs += [smem, vmem, vmem, vmem]
    out_rows = row_len // WIN if edge else rows // WIN
    return pl.pallas_call(
        functools.partial(attention_kernel, edge, row_len, width, sent),
        out_shape=jax.ShapeDtypeStruct((out_rows, model_width), jnp.float32),
        in_specs=specs,
        out_specs=vmem,
        scratch_shapes=[
            pltpu.VMEM((WIN, rows // WIN, width), jnp.bfloat16),
            pltpu.VMEM(merge_weight.shape, jnp.bfloat16),
            pltpu.SemaphoreType.DMA,
        ],
        compiler_params=pltpu.CompilerParams(vmem_limit_bytes=28 << 20),
        cost_estimate=pl.CostEstimate(
            flops=rows * 512 * width * 6, bytes_accessed=qkv.size * 2, transcendentals=rows * 512 * 8
        ),
        name="edge_attention" if edge else "middle_attention",
    )(*operands)


def norm_pack_kernel(width, mine_ref, other_ref, gain_ref, bias_ref, target_ref, half_ref, out_ref):
    merged = mine_ref[...] + other_ref[...]
    model_width = merged.shape[1]
    mean = jnp.sum(merged, axis=1, keepdims=True) / model_width
    variance = jnp.sum(merged * merged, axis=1, keepdims=True) / model_width - mean * mean
    normed = (merged - mean) * lax.rsqrt(variance + EPS) * gain_ref[...] + bias_ref[...]
    normed = normed.astype(jnp.bfloat16)
    left, right = normed[:, :width], normed[:, model_width - width :]
    place = lax.broadcasted_iota(jnp.int32, (out_ref.shape[0], merged.shape[0]), 0)
    place = jnp.where(place == target_ref[...], 1.0, 0.0).astype(jnp.bfloat16)
    half = half_ref[0]

    @pl.when(half == 0)
    def _():
        out_ref[...] = jnp.dot(place, left, preferred_element_type=jnp.float32).astype(jnp.bfloat16)

    @pl.when(half != 0)
    def _():
        out_ref[...] = jnp.dot(place, right, preferred_element_type=jnp.float32).astype(jnp.bfloat16)


def norm_pack(mine, other, gain, bias, target, half, slots, width):
    vmem = pl.BlockSpec(memory_space=pltpu.VMEM)
    return pl.pallas_call(
        functools.partial(norm_pack_kernel, width),
        out_shape=jax.ShapeDtypeStruct((slots, width), jnp.bfloat16),
        in_specs=[vmem] * 5 + [pl.BlockSpec(memory_space=pltpu.SMEM)],
        out_specs=vmem,
        compiler_params=pltpu.CompilerParams(vmem_limit_bytes=32 << 20),
        name="norm_pack",
    )(mine, other, gain[None], bias[None], target[None], half)


def project_kernel(half_ref, mine_ref, other_ref, weight_ref, out_ref, routed):
    width, model_width = mine_ref.shape[1], routed.shape[1]

    def place(left, right):
        routed[:, :width] = left[...]
        routed[:, model_width - width :] = right[...]

    first = pl.program_id(0) == 0
    pl.when(jnp.logical_and(first, half_ref[0] == 0))(lambda: place(mine_ref, other_ref))
    pl.when(jnp.logical_and(first, half_ref[0] != 0))(lambda: place(other_ref, mine_ref))
    out_ref[...] = lax.dot_general(
        weight_ref[...], routed[...], (((1,), (1,)), ((), ())), preferred_element_type=jnp.float32
    ).astype(jnp.bfloat16)


def project(half, mine, other, weight):
    columns, model_width = weight.shape
    slots, width = mine.shape
    step = next(s for s in (352, 264, 176, 128, 64, 32, 16, columns) if columns % s == 0)
    return pl.pallas_call(
        project_kernel,
        grid=(columns // step,),
        out_shape=jax.ShapeDtypeStruct((columns, slots), jnp.bfloat16),
        in_specs=[
            pl.BlockSpec(memory_space=pltpu.SMEM),
            pl.BlockSpec((slots, width), lambda i: (0, 0)),
            pl.BlockSpec((slots, width), lambda i: (0, 0)),
            pl.BlockSpec((step, model_width), lambda i: (i, 0)),
        ],
        out_specs=pl.BlockSpec((step, slots), lambda i: (i, 0)),
        scratch_shapes=[pltpu.VMEM((slots, model_width), jnp.bfloat16)],
        compiler_params=pltpu.CompilerParams(vmem_limit_bytes=32 << 20),
        name="project",
    )(half, mine, other, weight)


def body(qkv, segments, links, owners, merge_weight, norm_gain, norm_bias, next_weight):
    row_len = qkv.shape[1]
    model_width = norm_gain.shape[0]
    tp_size = lax.axis_size("tp")
    seg_ids = segments[0]
    linked = links[0] > 0
    sent = row_len // 4
    turned = jnp.swapaxes(qkv, 1, 2)
    last_flag = jnp.logical_and(seg_ids == seg_ids[row_len - 1], linked)[row_len - sent :]
    first_flag = (seg_ids == seg_ids[0])[:sent]

    def payload(pairs, flag):
        mark = jnp.broadcast_to(flag.astype(jnp.bfloat16)[None, None, :], (2, PACK, sent))
        return jnp.concatenate([pairs, mark], axis=1)

    prev = shifted(payload(turned[1:3, :, row_len - sent :], last_flag), "grp", 1)
    following = shifted(payload(turned[1:3, :, :sent], first_flag), "grp", -1)
    middle = run_attention(False, turned, segments, merge_weight, sent, None)
    partial_sum = run_attention(
        True, turned, segments, merge_weight, sent, (links, prev, following, middle)
    )
    merged_rows = row_len // WIN

    owner_ids = owners[0, :, 0]
    block_count = owner_ids.shape[0]
    group_count = lax.axis_size("grp")
    block_rows = merged_rows // block_count
    block_index = jnp.arange(block_count)
    earlier = block_index[:, None] > block_index[None, :]
    slot_rank = jnp.sum(
        jnp.logical_and(owner_ids[:, None] == owner_ids[None, :], earlier).astype(jnp.int32), axis=1
    )
    target = (owner_ids * CAP + slot_rank)[:, None] * block_rows + jnp.arange(block_rows)[None, :]
    target = target.reshape(merged_rows)
    slots = group_count * CAP * block_rows

    if tp_size == 2:
        half_index = lax.axis_index("tp")[None].astype(jnp.int32)
        other = swapped(partial_sum, "tp")
        part_width = -(-(model_width // 2) // TILE) * TILE
        packed = norm_pack(
            partial_sum, other, norm_gain, norm_bias, target, half_index, slots, part_width
        )
        packed = packed.reshape(group_count, CAP * block_rows, part_width)
        arrived = lax.all_to_all(packed, "grp", split_axis=0, concat_axis=0, tiled=True)
        arrived = arrived.reshape(slots, part_width)
        beside = swapped(arrived, "tp")
        projected = project(half_index, arrived, beside, next_weight.T)
        return projected.T[None]
    else:
        merged = lax.psum(partial_sum, "tp")
        mean = jnp.mean(merged, axis=1, keepdims=True)
        variance = jnp.mean(merged * merged, axis=1, keepdims=True) - mean * mean
        normed = (merged - mean) * lax.rsqrt(variance + EPS) * norm_gain + norm_bias
        normed = normed.astype(jnp.bfloat16)
        placing = (jnp.arange(slots)[:, None] == target[None, :]).astype(jnp.bfloat16)
        packed = jnp.dot(placing, normed, preferred_element_type=jnp.float32).astype(jnp.bfloat16)
        packed = packed.reshape(group_count, CAP * block_rows, model_width)
        routed = lax.all_to_all(packed, "grp", split_axis=0, concat_axis=0, tiled=True)
        routed = routed.reshape(slots, model_width)
    projected = jnp.dot(routed, next_weight, preferred_element_type=jnp.float32)
    return projected.astype(jnp.bfloat16)[None]


def solution(mesh):
    placed = (
        P(None, "grp", "tp"),
        P("grp", None),
        P("grp"),
        P("grp", None, None),
        P(None, "tp", None),
        P(),
        P(),
        P(None, "tp"),
    )
    return jax.shard_map(
        body, mesh=mesh, in_specs=placed, out_specs=P("grp", None, "tp"), check_vma=False
    )
```

```python
import functools
import math

import jax
import jax.numpy as jnp
from jax import lax
from jax.experimental import pallas as pl
from jax.experimental.pallas import tpu as pltpu
from jax.sharding import PartitionSpec as P

DH = 88
WIN = 4
CAP = 2
TILE = 128
PACK = 16
EPS = 1e-05
NEG = -1e30
SCALE2 = math.log2(math.e) / math.sqrt(DH)


def shifted(block, axis, distance):
    devices = range(lax.axis_size(axis))
    route = [(i - distance, i) for i in devices if i - distance in devices]
    return lax.ppermute(block, axis, route)


def swapped(block, axis):
    return lax.ppermute(block, axis, [(0, 1), (1, 0)])


def attend_heads(width, read_query, key_parts, bias_parts, value_parts, together=4):
    pieces = []
    for base in range(0, width // DH, together):
        lows = [head * DH for head in range(base, min(base + together, width // DH))]
        scores = []
        for low in lows:
            start, stop = low // TILE * TILE, min(width, -(-(low + DH) // TILE) * TILE)
            row = start + lax.broadcasted_iota(jnp.int32, (stop - start, 1), 0)
            inside = jnp.logical_and(row >= low, row < low + DH)
            query = read_query(start, stop)
            query = jnp.where(inside, query.astype(jnp.float32), 0.0).astype(jnp.bfloat16)
            scores.append(
                [jnp.dot(keys(start, stop), query, preferred_element_type=jnp.float32) for keys in key_parts]
            )
        scores = [[part * SCALE2 + bias for part, bias in zip(parts, bias_parts)] for parts in scores]
        tops = [
            functools.reduce(jnp.maximum, [jnp.max(part, axis=0, keepdims=True) for part in parts])
            for parts in scores
        ]
        weights = [[jnp.exp2(part - top) for part in parts] for parts, top in zip(scores, tops)]
        scales = [
            1.0 / functools.reduce(jnp.add, [jnp.sum(part, axis=0, keepdims=True) for part in parts])
            for parts in weights
        ]
        weights = [
            [(part * scale).astype(jnp.bfloat16) for part in parts] for parts, scale in zip(weights, scales)
        ]
        for low, parts in zip(lows, weights):
            start, stop = low // PACK * PACK, -(-(low + DH) // PACK) * PACK
            terms = [
                jnp.dot(values(start, stop), part, preferred_element_type=jnp.float32)
                for part, values in zip(parts, value_parts)
            ]
            pieces.append(functools.reduce(jnp.add, terms)[low - start : low - start + DH])
    return jnp.concatenate(pieces, axis=0)


def attention_kernel(edge, row_len, width, sent, *refs):
    if edge:
        seg_smem, qkv_hbm, seg_row, seg_col, merge_hbm, links, prev, following, middle, out = refs[:10]
    else:
        seg_smem, qkv_hbm, seg_row, seg_col, merge_hbm, out = refs[:6]
    attended, merge_vmem, merge_sem, qkv, qkv_sem, turned_keys, turned_sides = refs[-7:]
    tiles = row_len // TILE
    edge_tiles = sent // TILE
    tokens = TILE // WIN
    fetch = pltpu.make_async_copy(merge_hbm, merge_vmem, merge_sem)
    load = pltpu.make_async_copy(qkv_hbm, qkv, qkv_sem)
    load.start()
    fetch.start()
    if edge:
        for side, source in enumerate((prev, following)):
            for at in range(0, sent, TILE):
                turned_sides[side, at : at + TILE, :] = source[0, :width, at : at + TILE].T
    load.wait()

    @pl.loop(0, tiles)
    def _(tile):
        at = pl.multiple_of(tile * TILE, TILE)
        turned_keys[pl.ds(at, TILE), :] = qkv[1, :, pl.ds(at, TILE)].T

    ordered = lax.broadcasted_iota(jnp.int32, (TILE, TILE), 0)
    ordered = (ordered % tokens) * WIN + ordered // tokens
    order = (ordered == lax.broadcasted_iota(jnp.int32, (TILE, TILE), 1)).astype(jnp.float32)
    order = order.astype(jnp.bfloat16)

    def one(tile, out_row, neighbour):
        first = seg_smem[0, tile * TILE]
        last = seg_smem[0, tile * TILE + TILE - 1]
        begin, stop = jnp.int32(0), jnp.int32(0)
        for other in range(tiles):
            begin += (seg_smem[0, other * TILE + TILE - 1] < first).astype(jnp.int32)
            stop += (seg_smem[0, other * TILE] <= last).astype(jnp.int32)
        needed = stop - begin
        query_at = pl.multiple_of(tile * TILE, TILE)
        query_ids = seg_row[pl.ds(tile, 1), :]

        def run(count):
            key_at = pl.multiple_of(jnp.minimum(begin, tiles - count) * TILE, TILE)
            key_ids = seg_col[pl.ds(key_at, count * TILE), :]
            bias_parts = [jnp.where(key_ids == query_ids, 0.0, NEG)]
            key_parts = [lambda a, b: turned_keys[pl.ds(key_at, count * TILE), a:b]]
            value_parts = [lambda a, b: qkv[2, a:b, pl.ds(key_at, count * TILE)]]
            if neighbour is not None:
                side, source, segment, open_link = neighbour
                marks = jnp.transpose(source[0, width : width + PACK, :].astype(jnp.float32))[:, :1]
                wanted = jnp.logical_and(query_ids == segment, open_link).astype(jnp.float32)
                bias_parts.append(jnp.where(marks * wanted > 0.5, 0.0, NEG))
                key_parts.append(lambda a, b: turned_sides[side, :, a:b])
                value_parts.append(lambda a, b: source[1, a:b, :])
            mixed = attend_heads(
                width,
                lambda a, b: qkv[0, a:b, pl.ds(query_at, TILE)],
                key_parts,
                bias_parts,
                value_parts,
            )
            turned = lax.dot_general(
                order,
                mixed.astype(jnp.bfloat16),
                (((1,), (1,)), ((), ())),
                preferred_element_type=jnp.float32,
            ).astype(jnp.bfloat16)
            for j in range(WIN):
                attended[j, pl.ds(out_row, tokens), :] = turned[j * tokens : (j + 1) * tokens]

        sizes = [size for size in (2, 3, 4) if size < tiles] + [tiles]
        floor = 0
        for size in sizes:
            pl.when(jnp.logical_and(needed > floor, needed <= size))(functools.partial(run, size))
            floor = size

    if edge:
        @pl.loop(0, edge_tiles)
        def _(tile):
            one(tile, pl.multiple_of(tile * tokens, tokens), (0, prev, seg_smem[0, 0], True))

        @pl.loop(0, edge_tiles)
        def _(step):
            one(
                tiles - edge_tiles + step,
                pl.multiple_of((edge_tiles + step) * tokens, tokens),
                (1, following, seg_smem[0, row_len - 1], links[0] > 0),
            )
    else:
        @pl.loop(edge_tiles, tiles - edge_tiles)
        def _(tile):
            one(tile, pl.multiple_of((tile - edge_tiles) * tokens, tokens), None)

    fetch.wait()
    merged = jnp.dot(attended[0], merge_vmem[0], preferred_element_type=jnp.float32)
    for j in range(1, WIN):
        merged += jnp.dot(attended[j], merge_vmem[j], preferred_element_type=jnp.float32)
    if edge:
        half = merged.shape[0] // 2
        out[:half, :] = merged[:half]
        out[half : half + middle.shape[0], :] = middle[...]
        out[half + middle.shape[0] :, :] = merged[half:]
    else:
        out[...] = merged


def run_attention(edge, qkv, segments, merge_weight, sent, extra):
    width, row_len = qkv.shape[1:]
    model_width = merge_weight.shape[2]
    rows = 2 * sent if edge else row_len - 2 * sent
    smem = pl.BlockSpec(memory_space=pltpu.SMEM)
    vmem = pl.BlockSpec(memory_space=pltpu.VMEM)
    operands = [
        segments,
        qkv,
        segments.reshape(row_len // TILE, TILE),
        segments.reshape(row_len, 1),
        merge_weight,
    ]
    hbm = pl.BlockSpec(memory_space=pltpu.HBM)
    specs = [smem, hbm, vmem, vmem, hbm]
    if edge:
        operands += list(extra)
        specs += [smem, vmem, vmem, vmem]
    out_rows = row_len // WIN if edge else rows // WIN
    return pl.pallas_call(
        functools.partial(attention_kernel, edge, row_len, width, sent),
        out_shape=jax.ShapeDtypeStruct((out_rows, model_width), jnp.float32),
        in_specs=specs,
        out_specs=vmem,
        scratch_shapes=[
            pltpu.VMEM((WIN, rows // WIN, width), jnp.bfloat16),
            pltpu.VMEM(merge_weight.shape, jnp.bfloat16),
            pltpu.SemaphoreType.DMA,
            pltpu.VMEM(qkv.shape, jnp.bfloat16),
            pltpu.SemaphoreType.DMA,
            pltpu.VMEM((row_len, width), jnp.bfloat16),
            pltpu.VMEM((2, sent, width), jnp.bfloat16),
        ],
        compiler_params=pltpu.CompilerParams(vmem_limit_bytes=40 << 20),
        cost_estimate=pl.CostEstimate(
            flops=rows * 512 * width * 6, bytes_accessed=qkv.size * 2, transcendentals=rows * 512 * 8
        ),
        name="edge_attention" if edge else "middle_attention",
    )(*operands)


def norm_pack_kernel(width, mine_ref, other_ref, gain_ref, bias_ref, target_ref, half_ref, out_ref):
    merged = mine_ref[...] + other_ref[...]
    model_width = merged.shape[1]
    mean = jnp.sum(merged, axis=1, keepdims=True) / model_width
    variance = jnp.sum(merged * merged, axis=1, keepdims=True) / model_width - mean * mean
    normed = (merged - mean) * lax.rsqrt(variance + EPS) * gain_ref[...] + bias_ref[...]
    normed = normed.astype(jnp.bfloat16)
    left, right = normed[:, :width], normed[:, model_width - width :]
    place = lax.broadcasted_iota(jnp.int32, (out_ref.shape[0], merged.shape[0]), 0)
    place = jnp.where(place == target_ref[...], 1.0, 0.0).astype(jnp.bfloat16)
    half = half_ref[0]

    @pl.when(half == 0)
    def _():
        out_ref[...] = jnp.dot(place, left, preferred_element_type=jnp.float32).astype(jnp.bfloat16)

    @pl.when(half != 0)
    def _():
        out_ref[...] = jnp.dot(place, right, preferred_element_type=jnp.float32).astype(jnp.bfloat16)


def norm_pack(mine, other, gain, bias, target, half, slots, width):
    vmem = pl.BlockSpec(memory_space=pltpu.VMEM)
    return pl.pallas_call(
        functools.partial(norm_pack_kernel, width),
        out_shape=jax.ShapeDtypeStruct((slots, width), jnp.bfloat16),
        in_specs=[vmem] * 5 + [pl.BlockSpec(memory_space=pltpu.SMEM)],
        out_specs=vmem,
        compiler_params=pltpu.CompilerParams(vmem_limit_bytes=32 << 20),
        name="norm_pack",
    )(mine, other, gain[None], bias[None], target[None], half)


def project_kernel(half_ref, mine_ref, other_ref, weight_ref, out_ref, routed):
    width, model_width = mine_ref.shape[1], routed.shape[1]

    def place(left, right):
        routed[:, :width] = left[...]
        routed[:, model_width - width :] = right[...]

    first = pl.program_id(0) == 0
    pl.when(jnp.logical_and(first, half_ref[0] == 0))(lambda: place(mine_ref, other_ref))
    pl.when(jnp.logical_and(first, half_ref[0] != 0))(lambda: place(other_ref, mine_ref))
    out_ref[...] = lax.dot_general(
        weight_ref[...], routed[...], (((1,), (1,)), ((), ())), preferred_element_type=jnp.float32
    ).astype(jnp.bfloat16)


def project(half, mine, other, weight):
    columns, model_width = weight.shape
    slots, width = mine.shape
    step = next(s for s in (352, 264, 176, 128, 64, 32, 16, columns) if columns % s == 0)
    return pl.pallas_call(
        project_kernel,
        grid=(columns // step,),
        out_shape=jax.ShapeDtypeStruct((columns, slots), jnp.bfloat16),
        in_specs=[
            pl.BlockSpec(memory_space=pltpu.SMEM),
            pl.BlockSpec((slots, width), lambda i: (0, 0)),
            pl.BlockSpec((slots, width), lambda i: (0, 0)),
            pl.BlockSpec((step, model_width), lambda i: (i, 0)),
        ],
        out_specs=pl.BlockSpec((step, slots), lambda i: (i, 0)),
        scratch_shapes=[pltpu.VMEM((slots, model_width), jnp.bfloat16)],
        compiler_params=pltpu.CompilerParams(vmem_limit_bytes=56 << 20),
        name="project",
    )(half, mine, other, weight)


def body(qkv, segments, links, owners, merge_weight, norm_gain, norm_bias, next_weight):
    row_len = qkv.shape[1]
    model_width = norm_gain.shape[0]
    tp_size = lax.axis_size("tp")
    seg_ids = segments[0]
    linked = links[0] > 0
    sent = row_len // 4
    turned = jnp.swapaxes(qkv, 1, 2)
    last_flag = jnp.logical_and(seg_ids == seg_ids[row_len - 1], linked)[row_len - sent :]
    first_flag = (seg_ids == seg_ids[0])[:sent]

    def payload(pairs, flag):
        mark = jnp.broadcast_to(flag.astype(jnp.bfloat16)[None, None, :], (2, PACK, sent))
        return jnp.concatenate([pairs, mark], axis=1)

    prev = shifted(payload(turned[1:3, :, row_len - sent :], last_flag), "grp", 1)
    following = shifted(payload(turned[1:3, :, :sent], first_flag), "grp", -1)
    middle = run_attention(False, turned, segments, merge_weight, sent, None)
    partial_sum = run_attention(
        True, turned, segments, merge_weight, sent, (links, prev, following, middle)
    )
    merged_rows = row_len // WIN

    owner_ids = owners[0, :, 0]
    block_count = owner_ids.shape[0]
    group_count = lax.axis_size("grp")
    block_rows = merged_rows // block_count
    block_index = jnp.arange(block_count)
    earlier = block_index[:, None] > block_index[None, :]
    slot_rank = jnp.sum(
        jnp.logical_and(owner_ids[:, None] == owner_ids[None, :], earlier).astype(jnp.int32), axis=1
    )
    target = (owner_ids * CAP + slot_rank)[:, None] * block_rows + jnp.arange(block_rows)[None, :]
    target = target.reshape(merged_rows)
    slots = group_count * CAP * block_rows

    if tp_size == 2:
        half_index = lax.axis_index("tp")[None].astype(jnp.int32)
        other = swapped(partial_sum, "tp")
        part_width = -(-(model_width // 2) // TILE) * TILE
        packed = norm_pack(
            partial_sum, other, norm_gain, norm_bias, target, half_index, slots, part_width
        )
        packed = packed.reshape(group_count, CAP * block_rows, part_width)
        arrived = lax.all_to_all(packed, "grp", split_axis=0, concat_axis=0, tiled=True)
        arrived = arrived.reshape(slots, part_width)
        beside = swapped(arrived, "tp")
        projected = project(half_index, arrived, beside, next_weight.T)
        return projected.T[None]
    else:
        merged = lax.psum(partial_sum, "tp")
        mean = jnp.mean(merged, axis=1, keepdims=True)
        variance = jnp.mean(merged * merged, axis=1, keepdims=True) - mean * mean
        normed = (merged - mean) * lax.rsqrt(variance + EPS) * norm_gain + norm_bias
        normed = normed.astype(jnp.bfloat16)
        placing = (jnp.arange(slots)[:, None] == target[None, :]).astype(jnp.bfloat16)
        packed = jnp.dot(placing, normed, preferred_element_type=jnp.float32).astype(jnp.bfloat16)
        packed = packed.reshape(group_count, CAP * block_rows, model_width)
        routed = lax.all_to_all(packed, "grp", split_axis=0, concat_axis=0, tiled=True)
        routed = routed.reshape(slots, model_width)
    projected = jnp.dot(routed, next_weight, preferred_element_type=jnp.float32)
    return projected.astype(jnp.bfloat16)[None]


def solution(mesh):
    placed = (
        P(None, "grp", "tp"),
        P("grp", None),
        P("grp"),
        P("grp", None, None),
        P(None, "tp", None),
        P(),
        P(),
        P(None, "tp"),
    )
    return jax.shard_map(
        body, mesh=mesh, in_specs=placed, out_specs=P("grp", None, "tp"), check_vma=False
    )
```
